32 devices in a mesh: pipe: 4 (over y, x), ctx: 8 (over z, core).
Axes of the slice: x: 2, y: 2, z: 4, core: 2. Of those that a mesh axis runs over, the one named last changes fastest.
Arguments:
- tokens: bfloat16 [4, 1024, 8192], P('pipe', 'ctx')
- queries: bfloat16 [4, 1024, 4096], P('pipe', 'ctx')
- key_weight: bfloat16 [8192, 512], P(('pipe', 'ctx'))
- value_weight: bfloat16 [8192, 512], P(('pipe', 'ctx')), may hold values from -0.0625 to 0.0625
- block_order: int32 [16], replicated, may hold values from 0 to 15, as said below
Outputs:
- attended: bfloat16 [4, 1024, 4096], P('pipe', 'ctx')
The draws below stay inside these ranges and needn't reach their ends.
Inputs may be any that keep to these rules, and one draw needn't show every extreme that they name: `block_order`: each of the 16 half-blocks appears once.
All inputs are finite; a program needn't handle non-finite values.
Results may differ from the reference program's by a relative error of at most 0.0056.
The reference program's roundings to bfloat16 on the way count: a program that leaves them out, or rounds other values in their place, can miss the bound.
Values may be sent and summed in bfloat16 or wider, within the bound.
A program may use at most 64 MiB of HBM per device.

```python
import jax
import jax.numpy as jnp
from jax import lax

MODEL_WIDTH = 8192
QUERY_HEADS = 32
KEY_VALUE_HEADS = 4
HEAD_SIZE = 128
HALF = 64
HALVES = 16
SEQUENCE_TOKENS = 1024
MICRO = 4
QUERY_GROUP = 8
KVW = 512


def order_of(key):
    return jax.random.permutation(jax.random.fold_in(key, 11), HALVES).astype(jnp.int32)


def key_matrix(key):
    return jax.random.normal(jax.random.fold_in(key, 21), (MODEL_WIDTH, KEY_VALUE_HEADS * HEAD_SIZE), jnp.float32) * MODEL_WIDTH ** (-0.5)


def draw_block_order(key, part):
    return order_of(key)


def draw_key_weight(key, part):
    return key_matrix(key).astype(jnp.bfloat16)


def draw_tokens(key, part):
    base = jnp.clip(jax.random.normal(jax.random.fold_in(key, 41), (MICRO, SEQUENCE_TOKENS, MODEL_WIDTH), jnp.float32), -6.0, 6.0)
    return base.astype(jnp.bfloat16)


def draw_queries(key, part):
    base = jnp.clip(jax.random.normal(jax.random.fold_in(key, 43), (MICRO, SEQUENCE_TOKENS, QUERY_HEADS * HEAD_SIZE), jnp.float32), -6.0, 6.0)
    return base.astype(jnp.bfloat16)


def steps_of(own_key, shape, cuts, smallest, high):
    loudness = 1.0
    for axis_at, parts in cuts:
        steps = jax.random.uniform(jax.random.fold_in(jax.random.fold_in(own_key, 6), axis_at), (parts,), jnp.float32, smallest / len(cuts), high / len(cuts))
        loudness = loudness * jnp.repeat(jnp.exp(steps), shape[axis_at] // parts).reshape((-1,) + (1,) * (len(shape) - 1 - axis_at))
    return loudness


def scatter_about(rng, dims, width, reach, pieces=(), held_as=jnp.bfloat16):
    result = jax.random.normal(rng, dims, jnp.float32) * width
    if len(pieces) > 0:
        result = steps_of(rng, dims, pieces, -0.22, 0.18) * result
    return jnp.clip(result, min=-reach, max=reach).astype(held_as)


def setup_inputs(seed: int = 0) -> dict:
    arg_keys = jax.random.split(jax.random.key(seed), 6)
    tokens = draw_tokens(jax.random.fold_in(arg_keys[5], 71), 0)
    queries = draw_queries(jax.random.fold_in(arg_keys[5], 71), 0)
    key_weight = draw_key_weight(jax.random.fold_in(arg_keys[5], 71), 0)
    value_weight = scatter_about(arg_keys[3], (MODEL_WIDTH, KVW), MODEL_WIDTH ** -0.5, 0.0625, ((0, 32),))
    block_order = draw_block_order(jax.random.fold_in(arg_keys[5], 71), 0)
    return dict(tokens=tokens, queries=queries, key_weight=key_weight, value_weight=value_weight, block_order=block_order)


def reference(tokens, queries, key_weight, value_weight, block_order):
    position = jnp.repeat(block_order * HALF, HALF) + jnp.tile(jnp.arange(HALF, dtype=jnp.int32), HALVES)
    allowed = position[None, :] <= position[:, None]
    scale = 1.0 / (HEAD_SIZE ** 0.5)

    def one_batch(pair):
        hidden, query_rows = pair
        key_rows = jnp.dot(hidden, key_weight, preferred_element_type=jnp.float32).astype(jnp.bfloat16)
        value_rows = jnp.dot(hidden, value_weight, preferred_element_type=jnp.float32).astype(jnp.bfloat16)
        query_heads = query_rows.reshape(SEQUENCE_TOKENS, QUERY_HEADS, HEAD_SIZE).transpose(1, 0, 2)
        key_head_rows = jnp.repeat(key_rows.reshape(SEQUENCE_TOKENS, KEY_VALUE_HEADS, HEAD_SIZE).transpose(1, 0, 2), QUERY_GROUP, axis=0)
        value_head_rows = jnp.repeat(value_rows.reshape(SEQUENCE_TOKENS, KEY_VALUE_HEADS, HEAD_SIZE).transpose(1, 0, 2), QUERY_GROUP, axis=0)

        def one_head(triple):
            query_one, key_one, value_one = triple
            score = jnp.dot(query_one, key_one.T, preferred_element_type=jnp.float32) * scale
            largest = jnp.max(jnp.where(allowed, score, -jnp.inf), axis=1)
            expo = jnp.where(allowed, jnp.exp(score - largest[:, None]), 0.0)
            total = jnp.sum(expo, axis=1)
            weight = expo.astype(jnp.bfloat16)
            summed = jnp.dot(weight, value_one, preferred_element_type=jnp.float32)
            return (summed / total[:, None]).astype(jnp.bfloat16)

        heads_out = lax.map(one_head, (query_heads, key_head_rows, value_head_rows))
        return heads_out.transpose(1, 0, 2).reshape(SEQUENCE_TOKENS, QUERY_HEADS * HEAD_SIZE)

    return lax.map(one_batch, (tokens, queries))
```

```python
import functools

import jax
import jax.numpy as jnp
from jax import lax
from jax.experimental import pallas as pl
from jax.experimental.pallas import tpu as pltpu
from jax.sharding import PartitionSpec as P

HEAD_SIZE = 128
FIRST = 0
LOG2E = 1.4426950408889634
MESH = pl.DeviceIdType.MESH
PARTIAL = jnp.bfloat16


class Gather:
    def __init__(self, buf, rows, send, recv, lines):
        self.buf, self.rows, self.send_sems, self.recv_sems, self.lines = buf, rows, send, recv, lines
        self.me = lax.axis_index("ctx")
        self.line = self.me // 2
        self.core = self.me % 2
        self.partner = self.me + 1 - 2 * self.core

    def copy(self, g, origin, way):
        target = (self.me + 2, self.me - 2, self.partner)[way]
        return self.block_copy(g, origin, self.send_sems.at[g, origin // 2, way], target)

    def block_copy(self, g, origin, send_sem, target):
        block = self.buf.at[g, pl.ds(pl.multiple_of(origin * self.rows, self.rows), self.rows), :]
        return pltpu.make_async_remote_copy(
            src_ref=block,
            dst_ref=block,
            send_sem=send_sem,
            recv_sem=self.recv_sems.at[g, origin],
            device_id={"ctx": target},
            device_id_type=MESH,
        )

    def own(self, g):
        @pl.when(self.line < self.lines - 1)
        def _():
            self.copy(g, self.me, 0).start()

        @pl.when(self.line > 0)
        def _():
            self.copy(g, self.me, 1).start()

        self.copy(g, self.me, 2).start()

    def forward(self, g, start=1, stop=None):
        @pl.loop(start, self.lines if stop is None else stop)
        def _(hop):
            @pl.when(self.line >= hop)
            def _():
                origin = self.me - 2 * hop
                self.copy(g, origin, 2).wait_recv()

                @pl.when(self.line < self.lines - 1)
                def _():
                    self.copy(g, origin, 0).start()

                self.copy(g, origin, 2).start()

            @pl.when(self.line + hop < self.lines)
            def _():
                origin = self.me + 2 * hop
                self.copy(g, origin, 2).wait_recv()

                @pl.when(self.line > 0)
                def _():
                    self.copy(g, origin, 1).start()

                self.copy(g, origin, 2).start()

    def join(self, g):
        @pl.loop(0, self.lines)
        def _(line):
            self.copy(g, 2 * line + 1 - self.core, 2).wait_recv()

    def drain(self, chunks):
        @pl.loop(0, chunks)
        def _(g):
            @pl.loop(0, self.lines)
            def _(line):
                origin = 2 * line + self.core

                @pl.when((line <= self.line) & (self.line < self.lines - 1))
                def _():
                    self.copy(g, origin, 0).wait_send()

                @pl.when((line >= self.line) & (self.line > 0))
                def _():
                    self.copy(g, origin, 1).wait_send()

                self.copy(g, origin, 2).wait_send()


class Direct(Gather):
    def sent(self, g, step):
        line = lax.rem(self.line + step, self.lines)
        return self.block_copy(g, self.me, self.send_sems.at[g, step - 1, 0], 2 * line + self.core)

    def relay(self, g, line):
        return self.block_copy(g, 2 * line + self.core, self.send_sems.at[g, line, 1], self.partner)

    def own(self, g):
        for step in range(1, self.lines):
            self.sent(g, step).start()
        self.relay(g, self.line).start()

    def forward(self, g):
        @pl.loop(1, self.lines)
        def _(step):
            line = lax.rem(self.line + step, self.lines)
            self.relay(g, line).wait_recv()
            self.relay(g, line).start()

    def drain(self, chunks):
        @pl.loop(0, chunks)
        def _(g):
            @pl.loop(1, self.lines)
            def _(step):
                self.sent(g, step).wait_send()

            @pl.loop(0, self.lines)
            def _(line):
                self.relay(g, line).wait_send()


def kernel(
    pipes, ctxs, half,
    tok, qry, kw, vw, order, out,
    wbuf, xbuf, pout, pin, mine, kvbuf, qbuf, obuf,
    w_send, w_recv, kv_send, kv_recv, x_send, x_recv, p_send, p_recv, local, out_sem,
):
    chunks = wbuf.shape[0]
    rows = qbuf.shape[0]
    deep = kw.shape[0]
    slice_rows = xbuf.shape[2]
    lines = ctxs // 2
    group = qbuf.shape[1] // (chunks * HEAD_SIZE)
    seq = kvbuf.shape[1]
    pipe = lax.axis_index("pipe")
    me = lax.axis_index("ctx")
    weights = Gather(wbuf, deep, w_send, w_recv, lines)
    rows_kv = Direct(kvbuf, rows, kv_send, kv_recv, lines)

    def weight_copy(g, which):
        return pltpu.make_async_copy(
            (kw, vw)[which].at[:, pl.ds(g * HEAD_SIZE, HEAD_SIZE)],
            wbuf.at[g, pl.ds(pl.multiple_of(me * deep, deep), deep), pl.ds(which * HEAD_SIZE, HEAD_SIZE)],
            local.at[2 * g + which],
        )

    def own_tokens():
        return pltpu.make_async_copy(
            tok.at[0, :, pl.ds(pl.multiple_of(pipe * slice_rows, slice_rows), slice_rows)],
            xbuf.at[pipe],
            local.at[2 * chunks],
        )

    def own_queries():
        return pltpu.make_async_copy(qry.at[0], qbuf, local.at[2 * chunks + 1])

    def token_copy(d, to):
        return pltpu.make_async_remote_copy(
            src_ref=tok.at[0, :, pl.ds(pl.multiple_of(to * slice_rows, slice_rows), slice_rows)],
            dst_ref=xbuf.at[pipe],
            send_sem=x_send.at[d - 1],
            recv_sem=x_recv.at[d - 1],
            device_id={"pipe": to},
            device_id_type=MESH,
        )

    def token_wait(d):
        source = lax.rem(pipe + pipes - d, pipes)
        pltpu.make_async_remote_copy(
            src_ref=xbuf.at[source],
            dst_ref=xbuf.at[source],
            send_sem=x_send.at[d - 1],
            recv_sem=x_recv.at[d - 1],
            device_id={"pipe": source},
            device_id_type=MESH,
        ).wait_recv()

    def partial_copy(g, d):
        to = lax.rem(pipe + d, pipes)
        return pltpu.make_async_remote_copy(
            src_ref=pout.at[g, to],
            dst_ref=pin.at[g, d - 1],
            send_sem=p_send.at[g, d - 1],
            recv_sem=p_recv.at[g, d - 1],
            device_id={"pipe": to},
            device_id_type=MESH,
        )

    for g in range(chunks):
        for which in range(2):
            weight_copy(g, which).start()
    own_tokens().start()
    own_queries().start()

    barrier = pltpu.get_barrier_semaphore()
    for d in range(1, pipes):
        pl.semaphore_signal(barrier, inc=1, device_id={"pipe": lax.rem(pipe + d, pipes)}, device_id_type=MESH)
    pl.semaphore_signal(barrier, inc=1, device_id={"ctx": weights.partner}, device_id_type=MESH)
    for step in range(1, lines):
        to = 2 * lax.rem(weights.line + step, lines) + weights.core
        pl.semaphore_signal(barrier, inc=1, device_id={"ctx": to}, device_id_type=MESH)
    pl.semaphore_wait(barrier, pipes + lines - 1)

    def own_weights(g):
        weight_copy(g, 0).wait()
        weight_copy(g, 1).wait()
        weights.own(g)

    def multiply(g):
        weights.join(g)
        left = xbuf[...].reshape(pipes * rows, slice_rows)
        product = jnp.dot(left, wbuf[g], preferred_element_type=jnp.float32)
        pout[g] = product.reshape(pipes, rows, 2 * HEAD_SIZE).astype(pout.dtype)
        for d in range(1, pipes):
            partial_copy(g, d).start()
        for row in range(pipes):

            @pl.when(pipe == row)
            def _():
                mine[g] = product[row * rows : (row + 1) * rows]

    def total(g):
        value = mine[g]
        for d in range(1, pipes):
            partial_copy(g, d).wait_recv()
            value = value + pin[g, d - 1].astype(jnp.float32)
        kvbuf[g, pl.ds(pl.multiple_of(me * rows, rows), rows), :] = value.astype(jnp.bfloat16)
        rows_kv.own(g)

    lane = lax.broadcasted_iota(jnp.int32, (1, seq), 1)
    spot = jnp.zeros((1, seq), jnp.int32)
    for i in range(seq // half):
        spot = jnp.where(lane // half == i, order[i] * half, spot)
    key_position = spot + lane % half
    row = lax.broadcasted_iota(jnp.int32, (rows, 1), 0)
    spot = jnp.zeros((rows, 1), jnp.int32)
    per = rows // half
    for i in range(per):
        spot = jnp.where(row // half == i, order[me * per + i] * half, spot)
    own_position = spot + row % half

    factor = LOG2E / HEAD_SIZE**0.5

    def out_copy(g):
        columns = pl.ds(g * group * HEAD_SIZE, group * HEAD_SIZE)
        return pltpu.make_async_copy(obuf.at[:, columns], out.at[0, :, columns], out_sem.at[g])

    def attend(g):
        rows_kv.join(g)

        @pl.loop(0, group, unroll=8)
        def _(h):
            columns = pl.ds(pl.multiple_of((g * group + h) * HEAD_SIZE, HEAD_SIZE), HEAD_SIZE)
            keys = kvbuf[g, :, :HEAD_SIZE]
            values = kvbuf[g, :, HEAD_SIZE:]
            score = lax.dot_general(
                qbuf[:, columns], keys, (((1,), (1,)), ((), ())), preferred_element_type=jnp.float32
            )
            score = jnp.where(key_position <= own_position, score, -jnp.inf)
            largest = jnp.max(score, axis=1, keepdims=True)
            expo = jnp.exp2((score - largest) * factor)
            amount = jnp.sum(expo, axis=1, keepdims=True)
            summed = jnp.dot(expo.astype(jnp.bfloat16), values, preferred_element_type=jnp.float32)
            obuf[:, columns] = (summed / amount).astype(jnp.bfloat16)

        out_copy(g).start()

    def tokens_ready():
        own_tokens().wait()
        for d in range(1, pipes):
            token_wait(d)

    own_weights(0)
    for d in range(1, pipes):
        token_copy(d, lax.rem(pipe + d, pipes)).start()
    last = chunks - 1
    if last >= 1:
        own_weights(1)
    first = min(FIRST, last)
    for step in range(chunks + lines - 2):
        for hop in range(lines - 1, 0, -1):
            if 0 <= step - hop + 1 <= last:
                weights.forward(step - hop + 1, hop, hop + 1)
        if step + 2 <= last:
            own_weights(step + 2)
        done = step - (lines - 2)
        if done == first:
            tokens_ready()
            for g in range(done):
                multiply(g)
        if done >= first:
            if done == last and done >= 2:
                total(done - 2)
            multiply(done)
            if 2 <= done < last:
                total(done - 2)
    own_queries().wait()
    if last >= 1:
        total(last - 1)
    attended = max(last - 2, 0)
    for g in range(attended):
        rows_kv.forward(g)
        attend(g)
    total(last)
    for g in range(attended, last):
        rows_kv.forward(g)
        if g == last - 1:
            rows_kv.forward(last)
        attend(g)
    if last == 0:
        rows_kv.forward(last)
    attend(last)

    weights.drain(chunks)
    rows_kv.drain(chunks)
    for d in range(1, pipes):
        token_copy(d, lax.rem(pipe + d, pipes)).wait_send()
        for g in range(chunks):
            partial_copy(g, d).wait_send()
    for g in range(chunks):
        out_copy(g).wait()


def body(pipes, ctxs, tokens, queries, key_weight, value_weight, block_order):
    rows, width = tokens.shape[1:]
    deep, kv_width = key_weight.shape
    chunks = kv_width // HEAD_SIZE
    seq = rows * ctxs
    half = seq // block_order.shape[0]
    pair = 2 * HEAD_SIZE
    dma = pltpu.SemaphoreType.DMA
    any_space = pl.BlockSpec(memory_space=pl.ANY)
    return pl.pallas_call(
        functools.partial(kernel, pipes, ctxs, half),
        out_shape=jax.ShapeDtypeStruct(queries.shape, jnp.bfloat16),
        in_specs=[any_space] * 4 + [pl.BlockSpec(memory_space=pltpu.SMEM)],
        out_specs=any_space,
        scratch_shapes=[
            pltpu.VMEM((chunks, deep * ctxs, pair), jnp.bfloat16),
            pltpu.VMEM((pipes, rows, width // pipes), jnp.bfloat16),
            pltpu.VMEM((chunks, pipes, rows, pair), PARTIAL),
            pltpu.VMEM((chunks, pipes - 1, rows, pair), PARTIAL),
            pltpu.VMEM((chunks, rows, pair), jnp.float32),
            pltpu.VMEM((chunks, seq, pair), jnp.bfloat16),
            pltpu.VMEM(queries.shape[1:], jnp.bfloat16),
            pltpu.VMEM(queries.shape[1:], jnp.bfloat16),
            dma((chunks, ctxs // 2, 3)),
            dma((chunks, ctxs)),
            dma((chunks, ctxs // 2, 2)),
            dma((chunks, ctxs)),
            dma((pipes - 1,)),
            dma((pipes - 1,)),
            dma((chunks, pipes - 1)),
            dma((chunks, pipes - 1)),
            dma((2 * chunks + 2,)),
            dma((chunks,)),
        ],
        compiler_params=pltpu.CompilerParams(
            collective_id=0, has_side_effects=True, vmem_limit_bytes=60 * 1024 * 1024
        ),
    )(tokens, queries, key_weight, value_weight, block_order)


def solution(mesh):
    return jax.shard_map(
        functools.partial(body, mesh.shape["pipe"], mesh.shape["ctx"]),
        mesh=mesh,
        in_specs=(
            P("pipe", "ctx", None),
            P("pipe", "ctx", None),
            P(("pipe", "ctx"), None),
            P(("pipe", "ctx"), None),
            P(),
        ),
        out_specs=P("pipe", "ctx", None),
        check_vma=False,
    )
```
